256 devices in a mesh: rows: 8 (over y, core), vecs: 32 (over x, z).
Axes of the slice: x: 4, y: 4, z: 8, core: 2. Of those that a mesh axis runs over, the one named last changes fastest.
Arguments:
- vectors: float32 [4096, 8192], P('rows', 'vecs'), may hold values from -6 to 6
- reflectors: float32 [4, 16, 512, 256], P(None, 'rows', 'vecs'), may hold values from -0.4 to 1, as said below
Outputs:
- transformed: float32 [4096, 8192], P('rows', 'vecs')
The draws below stay inside these ranges and needn't reach their ends.
Inputs may be any that keep to these rules, and one draw needn't show every extreme that they name: reflectors[t, b] is unit lower trapezoidal: entry (i, j) is 1 where i == j and 0 where i < j.
All inputs are finite; a program needn't handle non-finite values.
Results may differ from the reference program's by a relative error of at most 0.00026.
Values sent between devices are 32-bit elements; how exact they have to be, the bound alone decides.
A program may use at most 128 MiB of HBM per device.

```python
import jax
import jax.numpy as jnp
import numpy as np
from jax import lax

SPREAD = 256
SEGMENTS = 4
BLOCKS_DEV = 2
BLOCKS = 16
ROW_COUNT = 4096
VEC_COUNT = 8192
N_ROWS = 8


def draw_reflectors(key, part):
    shape = (SEGMENTS, BLOCKS, 2 * SPREAD, SPREAD)
    row_index = lax.broadcasted_iota(jnp.int32, (2 * SPREAD, SPREAD), 0)
    col_index = lax.broadcasted_iota(jnp.int32, (2 * SPREAD, SPREAD), 1)
    raw = jnp.clip(0.06 * jax.random.normal(jax.random.fold_in(key, 13), shape, jnp.float32), -0.4, 0.4)
    lower_part = jnp.where(row_index == col_index, 1.0, 0.0).astype(jnp.float32)
    return jnp.where(row_index > col_index, raw, lower_part).astype(jnp.float32)


def block_levels(stream_key, dims, shards, low, high):
    level, own = 1.0, jax.random.fold_in(stream_key, 6)
    for axis_at, blocks in shards:
        draws = jnp.exp(jax.random.uniform(jax.random.fold_in(own, axis_at), (blocks,), jnp.float32, low / len(shards), high / len(shards)))
        level = level * jnp.repeat(draws, dims[axis_at] // blocks).reshape([-1 if axis == axis_at else 1 for axis in range(len(dims))])
    return level


def gaussian(stream_key, extent, spread, limit, shards=(), kind=jnp.bfloat16):
    values = spread * jax.random.normal(stream_key, extent, jnp.float32)
    if shards:
        values = values * block_levels(stream_key, extent, shards, -0.22, 0.18)
    return jnp.clip(values, -limit, limit).astype(kind)


def setup_inputs(seed: int = 0) -> dict:
    keys = jax.random.split(jax.random.key(seed), 3)
    vectors = gaussian(keys[0], (ROW_COUNT, VEC_COUNT), 1.0, 6.0, ((0, 8), (1, 32)), jnp.float32)
    reflectors = draw_reflectors(jax.random.fold_in(keys[2], 71), 0)
    return {"vectors": vectors, "reflectors": reflectors}


def invert_upper(matrix):
    size = matrix.shape[-1]
    if size == 1:
        return 1.0 / matrix
    half = size // 2
    upper_left = matrix[:, :half, :half]
    corner = matrix[:, :half, half:]
    lower_right = matrix[:, half:, half:]
    if half * 2 == size:
        count = matrix.shape[0]
        both = invert_upper(jnp.concatenate([upper_left, lower_right], axis=0))
        left_inverse = both[:count]
        right_inverse = both[count:]
    else:
        left_inverse = invert_upper(upper_left)
        right_inverse = invert_upper(lower_right)
    middle = jnp.einsum("bij,bjk->bik", corner, right_inverse, precision=lax.Precision.HIGHEST)
    middle = -jnp.einsum("bij,bjk->bik", left_inverse, middle, precision=lax.Precision.HIGHEST)
    zeros_block = jnp.zeros((matrix.shape[0], size - half, half), matrix.dtype)
    top = jnp.concatenate([left_inverse, middle], axis=2)
    bottom = jnp.concatenate([zeros_block, right_inverse], axis=2)
    return jnp.concatenate([top, bottom], axis=1)


def make_factor(gram):
    return jnp.triu(gram, 1) + 0.5 * jnp.diag(jnp.diagonal(gram))


def reflect(window_rows, vblock, inverse):
    products = jnp.dot(vblock.T, window_rows, precision=lax.Precision.HIGHEST)
    solved = jnp.dot(inverse, products, precision=lax.Precision.HIGHEST)
    return window_rows - jnp.dot(vblock, solved, precision=lax.Precision.HIGHEST)


def reference(vectors, reflectors):
    ordering = []
    for sweep in range(SEGMENTS + N_ROWS - 1):
        for block in range(BLOCKS):
            moment = sweep - (N_ROWS - 1) + block // BLOCKS_DEV
            if 0 <= moment < SEGMENTS:
                ordering.append((moment, block))
    table = jnp.asarray(np.array(ordering, dtype=np.int32))
    padded = jnp.concatenate([vectors, jnp.zeros((SPREAD, vectors.shape[1]), vectors.dtype)], axis=0)

    def advance(index, current):
        moment = table[index, 0]
        block = table[index, 1]
        vblock = reflectors[moment, block]
        start = (block * SPREAD).astype(jnp.int32)
        window_rows = lax.dynamic_slice_in_dim(current, start, 2 * SPREAD, 0)
        gram = jnp.dot(vblock.T, vblock, precision=lax.Precision.HIGHEST)
        inverse = invert_upper(make_factor(gram)[None])[0]
        updated = reflect(window_rows, vblock, inverse)
        return lax.dynamic_update_slice_in_dim(current, updated, start, 0)

    result = lax.fori_loop(0, len(ordering), advance, padded)
    return result[:ROW_COUNT]
```

```python
import jax
import jax.numpy as jnp
from jax import lax
from jax.experimental import pallas as pl
from jax.experimental.pallas import tpu as pltpu
from jax.sharding import PartitionSpec as P

F32, BF16 = jnp.float32, jnp.bfloat16
MESH = pl.DeviceIdType.MESH
STEPS, UNITS = 4, 8
W, C = 256, 128
NX, NZ = 4, 8
ROWS = 8


def split(value):
    high = value.astype(BF16)
    return high, (value - high.astype(F32)).astype(BF16)


def dot(a, b):
    return jnp.dot(a, b, preferred_element_type=F32)


def product(a, b):
    return dot(a[0], b[0]) + (dot(a[0], b[1]) + dot(a[1], b[0]))


def base_inverse(gram, x, upper, eye):
    diagonal = jnp.where(eye, gram, 0.0)
    along = 2.0 / jnp.sum(diagonal, axis=0, keepdims=True)
    down = 2.0 / jnp.sum(diagonal, axis=1, keepdims=True)
    strict = jnp.where(upper, gram, 0.0)
    return strict, jnp.where(eye, along, jnp.where(x == 1, -strict * along * down, 0.0))


def double(stricts, inverses, x, half):
    mask = (x >= half) & (x < 2 * half)
    corners = [split(jnp.where(mask, s, 0.0)) for s in stricts]
    pairs = [split(m) for m in inverses]
    middles = [split(product(b, m)) for b, m in zip(corners, pairs)]
    return [m - product(p, q) for m, p, q in zip(inverses, pairs, middles)]


def kernel(
    vec, refl, out,
    G, VH, VL, TH, TL, ZH, ZL, UB, MB, RET, BEN, UPO, DNO, XB,
    lsem, osem, xs, xr, zs, zr, us, ur, ds, dr,
):
    row = lax.axis_index("rows")
    v = lax.axis_index("vecs")
    x, z = v // NZ, lax.rem(v, NZ)

    def at_x(rel):
        return {"vecs": lax.rem(x + rel, NX) * NZ + z}

    def at_z(d):
        return {"vecs": x * NZ + lax.rem(z + NZ + d, NZ)}

    def local(i):
        if i < 2:
            return pltpu.make_async_copy(
                refl.at[:, :, pl.ds((1 - i) * C, C)], G.at[:, 2 * x + i, z], lsem.at[i]
            )
        half, c = (i - 2) // 2, (i - 2) % 2
        source = vec.at[pl.ds(half * W, W), pl.ds(c * C, C)]
        return pltpu.make_async_copy(source, XB.at[c] if half else RET.at[0, c], lsem.at[i])

    for i in range(6):
        local(i).start()

    barrier = pltpu.get_barrier_semaphore()
    for rel in (1, 2, 3):
        pl.semaphore_signal(barrier, inc=1, device_id=at_x(rel), device_id_type=MESH)
    for d in (1, -1):
        pl.semaphore_signal(barrier, inc=1, device_id=at_z(d), device_id_type=MESH)
        pl.semaphore_signal(
            barrier, inc=1, device_id={"rows": lax.rem(row + ROWS + d, ROWS)}, device_id_type=MESH
        )
    for i in range(6):
        local(i).wait()
    pl.semaphore_wait(barrier, 7)

    def xcopy(u, rel, source):
        slot = G.at[u, pl.ds(2 * source, 2), z]
        return pltpu.make_async_remote_copy(
            slot, slot, xs.at[u, rel - 1], xr.at[u, rel - 1], device_id=at_x(rel), device_id_type=MESH
        )

    def zcopy(u, d, k, source):
        slot = G.at[u, pl.ds(1, 7), source]
        way = 0 if d == 1 else 1
        return pltpu.make_async_remote_copy(
            slot, slot, zs.at[u, way, k - 1], zr.at[u, way, k - 1], device_id=at_z(d), device_id_type=MESH
        )

    def zsend(u, d, k):
        return zcopy(u, d, k, lax.rem(z + NZ - d * (k - 1), NZ))

    def zrecv(u, d, k):
        return zcopy(u, d, k, lax.rem(z + NZ - d * k, NZ))

    def hops(parity, d):
        return 4 if (d == 1) == (parity == 0) else 3

    def ready(u):
        for rel in (1, 2, 3):
            xcopy(u, rel, lax.rem(x + NX - rel, NX)).wait_recv()

    def arrive(u, parity, k):
        for d in (1, -1):
            if k == 0:
                zsend(u, d, 1).start()
            elif k <= hops(parity, d):
                zrecv(u, d, k).wait_recv()
                if k < hops(parity, d):
                    zsend(u, d, k + 1).start()

    for u in range(UNITS):
        for rel in (1, 3, 2):
            xcopy(u, rel, x).start()

    def wave(w, parity):
        for k in (4, 3, 2, 1, 0):
            u = w - k
            if isinstance(w, int):
                if 0 <= u < UNITS:
                    if k == 0:
                        ready(u)
                    arrive(u, u % 2, k)
            else:

                @pl.when(u < UNITS)
                def _(u=u, k=k):
                    if k == 0:
                        ready(u)
                    arrive(u, (parity + k) % 2, k)

    for w in range(4):
        wave(w, None)

    ri = lax.broadcasted_iota(jnp.int32, (W, W), 0)
    ci = lax.broadcasted_iota(jnp.int32, (W, W), 1)

    def prepare_first(t):
        stricts, inverses = [], []
        xor, upper, eye = ri ^ ci, ci > ri, ri == ci
        for j in range(2):
            u = 2 * t + j
            left = jnp.concatenate([G[u, 2 * i + 1].reshape(C, C) for i in range(NX)], axis=0)
            right = jnp.concatenate(
                [jnp.zeros((C, C), F32)] + [G[u, 2 * i].reshape(C, C) for i in range(1, NX)], axis=0
            )
            vh, vl = split(jnp.concatenate([left, right], axis=1))
            th, tl = vh.T, vl.T
            VH[u], VL[u] = vh, vl
            TH[j], TL[j] = th, tl
            strict, inverse = base_inverse(product((th, tl), (vh, vl)), xor, upper, eye)
            stricts.append(strict)
            inverses.append(inverse)
        for half in (2, 4, 8):
            inverses = double(stricts, inverses, xor, half)
        for j in range(2):
            UB[j], MB[j] = stricts[j], inverses[j]

    def prepare_second(t):
        stricts, inverses = [UB[0], UB[1]], [MB[0], MB[1]]
        for half in (16, 32, 64, 128):
            inverses = double(stricts, inverses, ri ^ ci, half)
        for j in range(2):
            zh, zl = split(product(split(inverses[j]), (TH[j], TL[j])))
            ZH[2 * t + j], ZL[2 * t + j] = zh, zl

    def up(t, c):
        return pltpu.make_async_remote_copy(
            UPO.at[t, c], BEN.at[t, c], us.at[t, c], ur.at[t, c],
            device_id={"rows": lax.rem(row + ROWS - 1, ROWS)}, device_id_type=MESH,
        )

    def down(t, c):
        return pltpu.make_async_remote_copy(
            DNO.at[t, c], RET.at[t + 1, c], ds.at[t, c], dr.at[t, c],
            device_id={"rows": lax.rem(row + 1, ROWS)}, device_id_type=MESH,
        )

    def solved_of(u, top, bottom):
        (th, tl), (bh, bl) = split(top), split(bottom)
        rh = jnp.concatenate([th, bh], axis=0)
        rl = jnp.concatenate([tl, bl], axis=0)
        wide = dot(ZH[u], jnp.concatenate([rh, rl], axis=1))
        return split(wide[:, :C] + (wide[:, C:] + dot(ZL[u], rh)))

    def change(u, start, solved):
        wide = dot(VH[u, start : start + W], jnp.concatenate(solved, axis=1))
        return wide[:, :C] + (wide[:, C:] + dot(VL[u, start : start + W], solved[0]))

    def even(t):
        u = 2 * t
        for c in range(2):

            @pl.when((row > 0) & (t > 0))
            def _():
                down(t - 1, c).wait_recv()

            top, bottom = RET[t, c], XB[c]
            solved = solved_of(u, top, bottom)
            top = top - change(u, 0, solved)

            @pl.when(row > 0)
            def _():
                UPO[t, c] = top
                up(t, c).start()

            @pl.when(row == 0)
            def _():
                RET[t + 1, c] = top

            XB[c] = bottom - change(u, W, solved)

    def odd(t):
        u = 2 * t + 1
        for c in range(2):

            @pl.when(row < ROWS - 1)
            def _():
                up(t, c).wait_recv()

            top, bottom = XB[c], BEN[t, c]
            solved = solved_of(u, top, bottom)
            bottom = bottom - change(u, W, solved)

            @pl.when(row < ROWS - 1)
            def _():
                DNO[t, c] = bottom
                down(t, c).start()

            @pl.when(row == ROWS - 1)
            def _():
                BEN[t + 1, c] = bottom

            XB[c] = top - change(u, 0, solved)

    @pl.when(row == ROWS - 1)
    def _():
        BEN[0] = jnp.zeros((2, W, C), F32)

    def tick(t, carry):
        pl.when(t > 0)(lambda: even(t - 1))

        @pl.when(t < STEPS)
        def _():
            wave(2 * t + 4, 0)
            wave(2 * t + 5, 1)
            prepare_first(t)

        pl.when(t > 0)(lambda: odd(t - 1))
        pl.when(t < STEPS)(lambda: prepare_second(t))
        return carry

    lax.fori_loop(0, STEPS + 1, tick, 0)

    def result(half, c):
        target = out.at[pl.ds(half * W, W), pl.ds(c * C, C)]
        return pltpu.make_async_copy(XB.at[c] if half else RET.at[STEPS, c], target, osem.at[half, c])

    for c in range(2):
        result(1, c).start()
    for c in range(2):

        @pl.when(row > 0)
        def _():
            down(STEPS - 1, c).wait_recv()

        result(0, c).start()

    def finish(u, carry):
        for rel in (1, 2, 3):
            xcopy(u, rel, x).wait_send()
        for d in (1, -1):
            for k in range(1, 4):
                zsend(u, d, k).wait_send()
        return carry

    lax.fori_loop(0, UNITS, finish, 0)

    def finish_pair(t, carry):
        zsend(2 * t, 1, 4).wait_send()
        zsend(2 * t + 1, -1, 4).wait_send()
        for c in range(2):
            pl.when(row > 0)(lambda: up(t, c).wait_send())
            pl.when(row < ROWS - 1)(lambda: down(t, c).wait_send())
        return carry

    lax.fori_loop(0, STEPS, finish_pair, 0)
    for half in range(2):
        for c in range(2):
            result(half, c).wait()


def local(vectors, reflectors):
    sem = pltpu.SemaphoreType.DMA
    anywhere = pl.BlockSpec(memory_space=pl.ANY)
    return pl.pallas_call(
        kernel,
        out_shape=jax.ShapeDtypeStruct(vectors.shape, F32),
        in_specs=[anywhere, anywhere],
        out_specs=anywhere,
        scratch_shapes=[
            pltpu.VMEM((UNITS, 2 * NX, NZ, 16, C), F32),
            pltpu.VMEM((UNITS, 2 * W, W), BF16),
            pltpu.VMEM((UNITS, 2 * W, W), BF16),
            pltpu.VMEM((2, W, 2 * W), BF16),
            pltpu.VMEM((2, W, 2 * W), BF16),
            pltpu.VMEM((UNITS, W, 2 * W), BF16),
            pltpu.VMEM((UNITS, W, 2 * W), BF16),
            pltpu.VMEM((2, W, W), F32),
            pltpu.VMEM((2, W, W), F32),
            pltpu.VMEM((STEPS + 1, 2, W, C), F32),
            pltpu.VMEM((STEPS + 1, 2, W, C), F32),
            pltpu.VMEM((STEPS, 2, W, C), F32),
            pltpu.VMEM((STEPS, 2, W, C), F32),
            pltpu.VMEM((2, W, C), F32),
            sem((6,)),
            sem((2, 2)),
            sem((UNITS, 3)),
            sem((UNITS, 3)),
            sem((UNITS, 2, 4)),
            sem((UNITS, 2, 4)),
            sem((STEPS, 2)),
            sem((STEPS, 2)),
            sem((STEPS, 2)),
            sem((STEPS, 2)),
        ],
        compiler_params=pltpu.CompilerParams(
            collective_id=0, has_side_effects=True, vmem_limit_bytes=56 * 2**20
        ),
    )(vectors, reflectors.reshape(UNITS, 16, W))


def solution(mesh):
    placed = (P("rows", "vecs"), P(None, "rows", "vecs", None))
    return jax.shard_map(
        local, mesh=mesh, in_specs=placed, out_specs=P("rows", "vecs"), check_vma=False
    )
```

```python
import jax
import jax.numpy as jnp
from jax import lax
from jax.experimental import pallas as pl
from jax.experimental.pallas import tpu as pltpu
from jax.sharding import PartitionSpec as P

F32, BF16 = jnp.float32, jnp.bfloat16
MESH = pl.DeviceIdType.MESH
STEPS, UNITS = 4, 8
W, C = 256, 128
NX, NZ = 4, 8
ROWS = 8


def split(value):
    high = value.astype(BF16)
    return high, (value - high.astype(F32)).astype(BF16)


def dot(a, b):
    return jnp.dot(a, b, preferred_element_type=F32)


def product(a, b):
    return dot(a[0], b[0]) + (dot(a[0], b[1]) + dot(a[1], b[0]))


def narrow_inverse(blocks):
    i = lax.broadcasted_iota(jnp.int32, (16, C), 0)
    lane = lax.broadcasted_iota(jnp.int32, (16, C), 1)
    j = lane % 16
    columns, accs = [], []
    for block in blocks:
        packed = block[:16]
        for k in range(1, C // 16):
            packed = jnp.where(lane // 16 == k, block[16 * k : 16 * k + 16], packed)
        packed = jnp.where(i < j, packed, jnp.where(i == j, 0.5 * packed, 0.0))
        columns.append(
            [jnp.take_along_axis(packed, lane - j + k, axis=1, mode="promise_in_bounds") for k in range(16)]
        )
        accs.append(jnp.where(i == j, 1.0, 0.0))
    for k in range(15, -1, -1):
        for n in range(len(blocks)):
            line = accs[n][k : k + 1] * (1.0 / columns[n][k][k : k + 1])
            accs[n] = jnp.where(i == k, line, accs[n] - columns[n][k] * line)
    ri = lax.broadcasted_iota(jnp.int32, (C, C), 0)
    ci = lax.broadcasted_iota(jnp.int32, (C, C), 1)
    return [jnp.where(ri // 16 == ci // 16, jnp.concatenate([a] * (C // 16), axis=0), 0.0) for a in accs]


def double(grams, inverses, half):
    ri = lax.broadcasted_iota(jnp.int32, (C, C), 0)
    ci = lax.broadcasted_iota(jnp.int32, (C, C), 1)
    mask = (ri ^ ci >= half) & (ri ^ ci < 2 * half) & (ri < ci)
    corners = [split(jnp.where(mask, g, 0.0)) for g in grams]
    pairs = [split(m) for m in inverses]
    middles = [split(product(b, m)) for b, m in zip(corners, pairs)]
    return [m - product(p, q) for m, p, q in zip(inverses, pairs, middles)]


def kernel(
    vec, refl, out,
    G, VH, VL, ZH, ZL, RET, BEN, UPO, DNO, XB,
    lsem, osem, gs, gr, us, ur, ds, dr,
):
    row = lax.axis_index("rows")
    v = lax.axis_index("vecs")
    x, z = v // NZ, lax.rem(v, NZ)

    def at_x(rel):
        return {"vecs": lax.rem(x + rel, NX) * NZ + z}

    turn = 1 - 2 * lax.rem(row, 2)

    def at_z(rel):
        return {"vecs": x * NZ + lax.rem(z + rel, NZ)}

    def local(i):
        if i < 2:
            return pltpu.make_async_copy(
                refl.at[:, :, pl.ds((1 - i) * C, C)], G.at[:, 2 * x + i, z], lsem.at[i]
            )
        half, c = (i - 2) // 2, (i - 2) % 2
        source = vec.at[pl.ds(half * W, W), pl.ds(c * C, C)]
        return pltpu.make_async_copy(source, XB.at[c] if half else RET.at[0, c], lsem.at[i])

    for i in range(6):
        local(i).start()

    barrier = pltpu.get_barrier_semaphore()
    for rel in (1, 2, 3):
        pl.semaphore_signal(barrier, inc=1, device_id=at_x(rel), device_id_type=MESH)
    for rel in range(1, NZ):
        pl.semaphore_signal(barrier, inc=1, device_id=at_z(rel), device_id_type=MESH)
    for rel in (1, ROWS - 1):
        beside = {"rows": lax.rem(row + rel, ROWS)}
        pl.semaphore_signal(barrier, inc=1, device_id=beside, device_id_type=MESH)
    for i in range(6):
        local(i).wait()
    pl.semaphore_wait(barrier, 12)

    def past_x(rel):
        return lax.rem(x + NX - rel, NX)

    def past_z(rel):
        return lax.rem(z + NZ - rel, NZ)

    def remote(slot, u, i, target):
        return pltpu.make_async_remote_copy(
            slot, slot, gs.at[u, i], gr.at[u, i], device_id=target, device_id_type=MESH
        )

    def xshard(u, rel, source):
        return remote(G.at[u, pl.ds(2 * source, 2), z], u, 6 + rel, at_x(rel))

    def zshard(u, rel, source):
        return remote(G.at[u, pl.ds(2 * x, 2), source], u, 5 + rel, at_z(rel))

    def xcolumn(u, i, side, rel, source):
        return remote(G.at[u, 2 * source + side], u, i, at_x(rel))

    def zrow(u, way, k, back):
        step = NZ + (turn if way == 0 else -turn)
        source = lax.rem(z + 5 * NZ - (step - NZ) * back, NZ)
        return remote(G.at[u, pl.ds(1, 7), source], u, k - 1 + 4 * way, at_z(step))

    HOPS = (4, 3)
    SIDES = tuple((side, rel) for rel in (1, 3, 2) for side in (1, 0))

    def unless_zero(side, source, run):
        if side == 1:
            run()
        else:
            pl.when(source != 0)(run)

    def by_row(u, k):
        if k == 0:
            for rel in (1, 3, 2):
                xshard(u, rel, past_x(rel)).wait_recv()
        for way in (0, 1):
            if 1 <= k <= HOPS[way]:
                zrow(u, way, k, k).wait_recv()
            if k < HOPS[way]:
                zrow(u, way, k + 1, k).start()

    def by_column(u, k):
        if k == 0:
            for rel in (1, 7, 2, 6, 3, 5, 4):
                zshard(u, rel, z).start()
        if k == 1:
            for rel in (1, 7, 2, 6, 3, 5, 4):
                zshard(u, rel, past_z(rel)).wait_recv()
            for i, (side, rel) in enumerate(SIDES):
                unless_zero(side, x, lambda: xcolumn(u, i, side, rel, x).start())
        if k == 2:
            for i, (side, rel) in enumerate(SIDES):
                unless_zero(side, past_x(rel), lambda: xcolumn(u, i, side, rel, past_x(rel)).wait_recv())

    def finish_by_row(u):
        for way in (0, 1):
            for k in range(1, HOPS[way] + 1):
                zrow(u, way, k, k - 1).wait_send()
        for rel in (1, 2, 3):
            xshard(u, rel, x).wait_send()

    def finish_by_column(u):
        for rel in range(1, NZ):
            zshard(u, rel, z).wait_send()
        for i, (side, rel) in enumerate(SIDES):
            unless_zero(side, x, lambda: xcolumn(u, i, side, rel, x).wait_send())

    by_column(0, 0)
    for u in (2, 4, 6):
        for rel in (1, 3, 2):
            xshard(u, rel, x).start()
    by_column(1, 0)
    by_column(0, 1)
    by_column(1, 1)
    by_row(2, 0)
    by_column(3, 0)
    by_row(2, 1)
    by_column(0, 2)

    def wave(s, events):
        for run, ahead, k in events:
            pl.when(s + ahead < UNITS)(lambda: run(s + ahead, k))

    AFTER_EVEN = ((by_row, 2, 3), (by_row, 4, 1), (by_column, 3, 1), (by_column, 5, 0), (by_column, 1, 2))
    AFTER_ODD = ((by_row, 3, 2), (by_row, 5, 0), (by_row, 1, 4))

    def prepare(u):
        left = jnp.concatenate([G[u, 2 * i + 1].reshape(C, C) for i in range(NX)], axis=0)
        right = jnp.concatenate(
            [jnp.zeros((C, C), F32)] + [G[u, 2 * i].reshape(C, C) for i in range(1, NX)], axis=0
        )
        vh, vl = split(jnp.concatenate([left, right], axis=1))
        th, tl = vh.T, vl.T
        VH[u], VL[u] = vh, vl
        upper = product((th[:C], tl[:C]), (vh, vl))
        lower = product((th[C:, C:], tl[C:, C:]), (vh[C:, C:], vl[C:, C:]))
        grams = [upper[:, :C], lower]
        inverses = narrow_inverse(grams)
        for half in (16, 32, 64):
            inverses = double(grams, inverses, half)
        (ah, al), (ch, cl) = split(inverses[0]), split(inverses[1])
        corner = product((ah, al), split(product(split(upper[:, C:]), (ch, cl))))
        bh, bl = split(-corner)
        wide = (jnp.concatenate([ah, bh], axis=1), jnp.concatenate([al, bl], axis=1))
        ZH[u, :C], ZL[u, :C] = split(product(wide, (th, tl)))
        ZH[u, C:], ZL[u, C:] = split(product((ch, cl), (th[C:], tl[C:])))

    def up(t, c):
        return pltpu.make_async_remote_copy(
            UPO.at[t, c], BEN.at[t, c], us.at[t, c], ur.at[t, c],
            device_id={"rows": lax.rem(row + ROWS - 1, ROWS)}, device_id_type=MESH,
        )

    def down(t, c):
        return pltpu.make_async_remote_copy(
            DNO.at[t, c], RET.at[t + 1, c], ds.at[t, c], dr.at[t, c],
            device_id={"rows": lax.rem(row + 1, ROWS)}, device_id_type=MESH,
        )

    def solved_of(u, top, bottom):
        (th, tl), (bh, bl) = split(top), split(bottom)
        rh = jnp.concatenate([th, bh], axis=0)
        rl = jnp.concatenate([tl, bl], axis=0)
        wide = dot(ZH[u], jnp.concatenate([rh, rl], axis=1))
        return split(wide[:, :C] + (wide[:, C:] + dot(ZL[u], rh)))

    def change(u, start, solved):
        wide = dot(VH[u, start : start + W], jnp.concatenate(solved, axis=1))
        return wide[:, :C] + (wide[:, C:] + dot(VL[u, start : start + W], solved[0]))

    def even(t):
        u = 2 * t
        for c in range(2):

            @pl.when((row > 0) & (t > 0))
            def _():
                down(t - 1, c).wait_recv()

            top, bottom = RET[t, c], XB[c]
            solved = solved_of(u, top, bottom)
            top = top - change(u, 0, solved)

            @pl.when(row > 0)
            def _():
                UPO[t, c] = top
                up(t, c).start()

            @pl.when(row == 0)
            def _():
                RET[t + 1, c] = top

            XB[c] = bottom - change(u, W, solved)

    def odd(t):
        u = 2 * t + 1
        for c in range(2):

            @pl.when(row < ROWS - 1)
            def _():
                up(t, c).wait_recv()

            top, bottom = XB[c], BEN[t, c]
            solved = solved_of(u, top, bottom)
            bottom = bottom - change(u, W, solved)

            @pl.when(row < ROWS - 1)
            def _():
                DNO[t, c] = bottom
                down(t, c).start()

            @pl.when(row == ROWS - 1)
            def _():
                BEN[t + 1, c] = bottom

            XB[c] = top - change(u, 0, solved)

    @pl.when(row == ROWS - 1)
    def _():
        BEN[0] = jnp.zeros((2, W, C), F32)

    def tick(t, carry):
        pl.when(t > 0)(lambda: even(t - 1))

        @pl.when(t > 0)
        def _():
            wave(2 * t - 2, AFTER_EVEN)
            prepare(2 * t - 1)

        pl.when(t > 0)(lambda: odd(t - 1))

        @pl.when(t < STEPS)
        def _():
            pl.when(t > 0)(lambda: wave(2 * t - 1, AFTER_ODD))
            prepare(2 * t)

        @pl.when(t == 0)
        def _():
            by_row(2, 2)
            by_row(4, 0)

        return carry

    lax.fori_loop(0, STEPS + 1, tick, 0)

    def result(half, c):
        target = out.at[pl.ds(half * W, W), pl.ds(c * C, C)]
        return pltpu.make_async_copy(XB.at[c] if half else RET.at[STEPS, c], target, osem.at[half, c])

    for c in range(2):
        result(1, c).start()
    for c in range(2):

        @pl.when(row > 0)
        def _():
            down(STEPS - 1, c).wait_recv()

        result(0, c).start()

    def finish_pair(t, carry):
        pl.when(t == 0)(lambda: finish_by_column(2 * t))
        pl.when(t != 0)(lambda: finish_by_row(2 * t))
        finish_by_column(2 * t + 1)
        for c in range(2):
            pl.when(row > 0)(lambda: up(t, c).wait_send())
            pl.when(row < ROWS - 1)(lambda: down(t, c).wait_send())
        return carry

    lax.fori_loop(0, STEPS, finish_pair, 0)
    for half in range(2):
        for c in range(2):
            result(half, c).wait()


def local(vectors, reflectors):
    sem = pltpu.SemaphoreType.DMA
    anywhere = pl.BlockSpec(memory_space=pl.ANY)
    return pl.pallas_call(
        kernel,
        out_shape=jax.ShapeDtypeStruct(vectors.shape, F32),
        in_specs=[anywhere, anywhere],
        out_specs=anywhere,
        scratch_shapes=[
            pltpu.VMEM((UNITS, 2 * NX, NZ, 16, C), F32),
            pltpu.VMEM((UNITS, 2 * W, W), BF16),
            pltpu.VMEM((UNITS, 2 * W, W), BF16),
            pltpu.VMEM((UNITS, W, 2 * W), BF16),
            pltpu.VMEM((UNITS, W, 2 * W), BF16),
            pltpu.VMEM((STEPS + 1, 2, W, C), F32),
            pltpu.VMEM((STEPS + 1, 2, W, C), F32),
            pltpu.VMEM((STEPS, 2, W, C), F32),
            pltpu.VMEM((STEPS, 2, W, C), F32),
            pltpu.VMEM((2, W, C), F32),
            sem((6,)),
            sem((2, 2)),
            sem((UNITS, 13)),
            sem((UNITS, 13)),
            sem((STEPS, 2)),
            sem((STEPS, 2)),
            sem((STEPS, 2)),
            sem((STEPS, 2)),
        ],
        compiler_params=pltpu.CompilerParams(
            collective_id=0, has_side_effects=True, vmem_limit_bytes=56 * 2**20
        ),
    )(vectors, reflectors.reshape(UNITS, 16, W))


def solution(mesh):
    placed = (P("rows", "vecs"), P(None, "rows", "vecs", None))
    return jax.shard_map(
        local, mesh=mesh, in_specs=placed, out_specs=P("rows", "vecs"), check_vma=False
    )
```

```python
import jax
import jax.numpy as jnp
from jax import lax
from jax.experimental import pallas as pl
from jax.experimental.pallas import tpu as pltpu
from jax.sharding import PartitionSpec as P

F32, BF16 = jnp.float32, jnp.bfloat16
MESH = pl.DeviceIdType.MESH
STEPS, UNITS = 4, 8
W, C = 256, 128
NX, NZ = 4, 8
ROWS = 8


def split(value):
    high = value.astype(BF16)
    return high, (value - high.astype(F32)).astype(BF16)


def dot(a, b):
    return jnp.dot(a, b, preferred_element_type=F32)


def product(a, b):
    return dot(a[0], b[0]) + (dot(a[0], b[1]) + dot(a[1], b[0]))


def square(a, b):
    right = jnp.concatenate(
        [jnp.concatenate([b[0], b[1]], axis=1), jnp.concatenate([b[0], jnp.zeros_like(b[0])], axis=1)], axis=0
    )
    both = dot(jnp.concatenate([a[0], a[1]], axis=1), right)
    return both[:, :C] + both[:, C:]


NARROW = 32


def narrow_inverse(blocks):
    i = lax.broadcasted_iota(jnp.int32, (NARROW, C), 0)
    lane = lax.broadcasted_iota(jnp.int32, (NARROW, C), 1)
    j = lane % NARROW
    packs, accs = [], []
    for block in blocks:
        packed = block[:NARROW]
        for k in range(1, C // NARROW):
            packed = jnp.where(lane // NARROW == k, block[NARROW * k : NARROW * (k + 1)], packed)
        packs.append(jnp.where(i < j, packed, jnp.where(i == j, 0.5 * packed, 0.0)))
        accs.append(jnp.where(i == j, 1.0, 0.0))
    for k in range(NARROW - 1, -1, -1):
        live = 8 * (k // 8 + 1)
        for n in range(len(blocks)):
            column = jnp.take_along_axis(
                packs[n][:live], (lane - j + k)[:live], axis=1, mode="promise_in_bounds"
            )
            line = accs[n][k : k + 1] * (1.0 / column[k : k + 1])
            changed = jnp.where(i[:live] == k, line, accs[n][:live] - column * line)
            accs[n] = jnp.concatenate([changed, accs[n][live:]], axis=0) if live < NARROW else changed
    ri = lax.broadcasted_iota(jnp.int32, (C, C), 0)
    ci = lax.broadcasted_iota(jnp.int32, (C, C), 1)
    inside = ri // NARROW == ci // NARROW
    return [jnp.where(inside, jnp.concatenate([a] * (C // NARROW), axis=0), 0.0) for a in accs]


def widen(grams, inverses):
    ri = lax.broadcasted_iota(jnp.int32, (C, C), 0)
    ci = lax.broadcasted_iota(jnp.int32, (C, C), 1)
    above = ri // NARROW < ci // NARROW
    diagonals = [split(m) for m in inverses]
    nils = [split(square(d, split(jnp.where(above, g, 0.0)))) for d, g in zip(diagonals, grams)]
    twice = [split(square(n, n)) for n in nils]
    nears = [m - square(n, d) for m, n, d in zip(inverses, nils, diagonals)]
    return [p + square(q, split(p)) for p, q in zip(nears, twice)]


def kernel(
    vec, refl, out,
    G, VH, VL, ZH, ZL, RET, BEN, UPO, DNO, XB,
    lsem, osem, fs, fr, gs, gr, us, ur, ds, dr,
):
    row = lax.axis_index("rows")
    v = lax.axis_index("vecs")
    x, z = v // NZ, lax.rem(v, NZ)

    def at_x(rel):
        return {"vecs": lax.rem(x + rel, NX) * NZ + z}

    turn = 1 - 2 * lax.rem(row, 2)

    def at_z(rel):
        return {"vecs": x * NZ + lax.rem(z + rel, NZ)}

    def local(i):
        if i < 2:
            return pltpu.make_async_copy(
                refl.at[:, :, pl.ds((1 - i) * C, C)], G.at[:, 2 * x + i, z], lsem.at[i]
            )
        half, c = (i - 2) // 2, (i - 2) % 2
        source = vec.at[pl.ds(half * W, W), pl.ds(c * C, C)]
        return pltpu.make_async_copy(source, XB.at[c] if half else RET.at[0, c], lsem.at[i])

    for i in range(6):
        local(i).start()

    barrier = pltpu.get_barrier_semaphore()
    for rel in (1, 2, 3):
        pl.semaphore_signal(barrier, inc=1, device_id=at_x(rel), device_id_type=MESH)
    for rel in range(1, NZ):
        pl.semaphore_signal(barrier, inc=1, device_id=at_z(rel), device_id_type=MESH)
    for rel in (1, ROWS - 1):
        beside = {"rows": lax.rem(row + rel, ROWS)}
        pl.semaphore_signal(barrier, inc=1, device_id=beside, device_id_type=MESH)
    for i in range(6):
        local(i).wait()
    pl.semaphore_wait(barrier, 12)

    def past_x(rel):
        return lax.rem(x + NX - rel, NX)

    def past_z(rel):
        return lax.rem(z + NZ - rel, NZ)

    def remote(slot, u, i, target):
        return pltpu.make_async_remote_copy(
            slot, slot, gs.at[u, i], gr.at[u, i], device_id=target, device_id_type=MESH
        )

    def xshard(u, rel, source):
        return remote(G.at[u, pl.ds(2 * source, 2), z], u, 6 + rel, at_x(rel))

    def zshard(u, rel, source):
        return remote(G.at[u, pl.ds(2 * x, 2), source], u, 5 + rel, at_z(rel))

    def xcolumn(u, i, side, rel, source):
        return remote(G.at[u, 2 * source + side], u, i, at_x(rel))

    def zrow(u, way, k, back):
        step = NZ + (turn if way == 0 else -turn)
        source = lax.rem(z + 5 * NZ - (step - NZ) * back, NZ)
        return remote(G.at[u, pl.ds(1, 7), source], u, k - 1 + 4 * way, at_z(step))

    HOPS = (4, 3)
    SIDES = tuple((side, rel) for rel in (1, 3, 2) for side in (1, 0))

    def unless_zero(side, source, run):
        if side == 1:
            run()
        else:
            pl.when(source != 0)(run)

    def by_row(u, k):
        if k == 0:
            for rel in (1, 3, 2):
                xshard(u, rel, past_x(rel)).wait_recv()
        for way in (0, 1):
            if 1 <= k <= HOPS[way]:
                zrow(u, way, k, k).wait_recv()
            if k < HOPS[way]:
                zrow(u, way, k + 1, k).start()

    def by_column(u, k):
        if k == 0:
            for rel in (1, 7, 2, 6, 3, 5, 4):
                zshard(u, rel, z).start()
        if k == 1:
            for rel in (1, 7, 2, 6, 3, 5, 4):
                zshard(u, rel, past_z(rel)).wait_recv()
            for i, (side, rel) in enumerate(SIDES):
                unless_zero(side, x, lambda: xcolumn(u, i, side, rel, x).start())
        if k == 2:
            for i, (side, rel) in enumerate(SIDES):
                unless_zero(side, past_x(rel), lambda: xcolumn(u, i, side, rel, past_x(rel)).wait_recv())

    def finish_by_row(u):
        for way in (0, 1):
            for k in range(1, HOPS[way] + 1):
                zrow(u, way, k, k - 1).wait_send()
        for rel in (1, 2, 3):
            xshard(u, rel, x).wait_send()

    def finish_by_column(u):
        for rel in range(1, NZ):
            zshard(u, rel, z).wait_send()
        for i, (side, rel) in enumerate(SIDES):
            unless_zero(side, x, lambda: xcolumn(u, i, side, rel, x).wait_send())

    ARRIVAL = (0, 1, 7, 2, 6, 3, 5, 4)

    def crossing(rel, along, source):
        i = 3 * along + rel - 1
        slot = G.at[0, pl.ds(2 * source, 2), past_z(along)]
        return pltpu.make_async_remote_copy(
            slot, slot, fs.at[i], fr.at[i], device_id=at_x(rel), device_id_type=MESH
        )

    for rel in (1, 3, 2):
        xshard(2, rel, x).start()
    by_column(0, 0)
    for rel in (1, 3, 2):
        crossing(rel, 0, x).start()
    by_row(2, 0)
    for along in ARRIVAL[1:]:
        zshard(0, along, past_z(along)).wait_recv()
        for rel in (1, 3, 2):
            crossing(rel, along, x).start()
    by_column(1, 0)
    for u in (4, 6):
        for rel in (1, 3, 2):
            xshard(u, rel, x).start()
    by_row(2, 1)
    by_column(3, 0)
    by_row(2, 2)
    for along in ARRIVAL:
        for rel in (1, 3, 2):
            crossing(rel, along, past_x(rel)).wait_recv()
    by_column(1, 1)

    def wave(s, events):
        for run, ahead, k in events:
            taken = (s + ahead < UNITS) & (s > 0) if (ahead, k) in ((2, 3),) else s + ahead < UNITS
            pl.when(taken)(lambda: run(s + ahead, k))

    AFTER_EVEN = ((by_row, 2, 3), (by_row, 4, 1), (by_column, 3, 1), (by_column, 5, 0), (by_column, 1, 2))
    AFTER_ODD = ((by_row, 3, 2), (by_row, 5, 0), (by_row, 1, 4))

    def prepare(u):
        left = jnp.concatenate([G[u, 2 * i + 1].reshape(C, C) for i in range(NX)], axis=0)
        right = jnp.concatenate(
            [jnp.zeros((C, C), F32)] + [G[u, 2 * i].reshape(C, C) for i in range(1, NX)], axis=0
        )
        vh, vl = split(jnp.concatenate([left, right], axis=1))
        th, tl = vh.T, vl.T
        VH[u], VL[u] = vh, vl
        upper = product((th[:C], tl[:C]), (vh, vl))
        both = dot(th[C:, C:], jnp.concatenate([vh[C:, C:], vl[C:, C:]], axis=1))
        lower = both[:, :C] + (both[:, C:] + dot(tl[C:, C:], vh[C:, C:]))
        grams = [upper[:, :C], lower]
        inverses = widen(grams, narrow_inverse(grams))
        (ah, al), (ch, cl) = split(inverses[0]), split(inverses[1])
        corner = square((ah, al), split(square(split(upper[:, C:]), (ch, cl))))
        bh, bl = split(-corner)
        wide = (jnp.concatenate([ah, bh], axis=1), jnp.concatenate([al, bl], axis=1))
        ZH[u, :C], ZL[u, :C] = split(product(wide, (th, tl)))
        ZH[u, C:], ZL[u, C:] = split(
            dot(jnp.concatenate([ch, cl], axis=1), jnp.concatenate([th[C:], th[C:]], axis=0)) + dot(ch, tl[C:])
        )

    def up(t, c):
        return pltpu.make_async_remote_copy(
            UPO.at[t, c], BEN.at[t, c], us.at[t, c], ur.at[t, c],
            device_id={"rows": lax.rem(row + ROWS - 1, ROWS)}, device_id_type=MESH,
        )

    def down(t, c):
        return pltpu.make_async_remote_copy(
            DNO.at[t, c], RET.at[t + 1, c], ds.at[t, c], dr.at[t, c],
            device_id={"rows": lax.rem(row + 1, ROWS)}, device_id_type=MESH,
        )

    def solved_of(u, top, bottom):
        (th, tl), (bh, bl) = split(top), split(bottom)
        rh = jnp.concatenate([th, bh], axis=0)
        rl = jnp.concatenate([tl, bl], axis=0)
        wide = dot(ZH[u], jnp.concatenate([rh, rl], axis=1))
        return split(wide[:, :C] + (wide[:, C:] + dot(ZL[u], rh)))

    def change(u, start, solved):
        wide = dot(VH[u, start : start + W], jnp.concatenate(solved, axis=1))
        return wide[:, :C] + (wide[:, C:] + dot(VL[u, start : start + W], solved[0]))

    def even(t):
        u = 2 * t
        for c in range(2):

            @pl.when((row > 0) & (t > 0))
            def _():
                down(t - 1, c).wait_recv()

            top, bottom = RET[t, c], XB[c]
            solved = solved_of(u, top, bottom)
            top = top - change(u, 0, solved)

            @pl.when(row > 0)
            def _():
                UPO[t, c] = top
                up(t, c).start()

            @pl.when(row == 0)
            def _():
                RET[t + 1, c] = top

            XB[c] = bottom - change(u, W, solved)

    def odd(t):
        u = 2 * t + 1
        for c in range(2):

            @pl.when(row < ROWS - 1)
            def _():
                up(t, c).wait_recv()

            top, bottom = XB[c], BEN[t, c]
            solved = solved_of(u, top, bottom)
            bottom = bottom - change(u, W, solved)

            @pl.when(row < ROWS - 1)
            def _():
                DNO[t, c] = bottom
                down(t, c).start()

            @pl.when(row == ROWS - 1)
            def _():
                BEN[t + 1, c] = bottom

            XB[c] = top - change(u, 0, solved)

    @pl.when(row == ROWS - 1)
    def _():
        BEN[0] = jnp.zeros((2, W, C), F32)

    def finish_first():
        for along in range(NZ):
            if along:
                zshard(0, along, z).wait_send()
            for rel in (1, 2, 3):
                crossing(rel, along, x).wait_send()

    def finish_gather(t, carry):
        pl.when(t == 0)(finish_first)
        pl.when(t != 0)(lambda: finish_by_row(2 * t))
        finish_by_column(2 * t + 1)
        return carry

    def tick(t, carry):
        pl.when(t > 0)(lambda: even(t - 1))

        @pl.when(t > 0)
        def _():
            wave(2 * t - 2, AFTER_EVEN)
            prepare(2 * t - 1)

        @pl.when(t == STEPS)
        def _():
            lax.fori_loop(0, STEPS, finish_gather, 0)

        pl.when(t > 0)(lambda: odd(t - 1))

        @pl.when(t < STEPS)
        def _():
            pl.when(t > 0)(lambda: wave(2 * t - 1, AFTER_ODD))
            prepare(2 * t)

        @pl.when(t == 0)
        def _():
            by_row(2, 3)
            by_row(4, 0)

        return carry

    lax.fori_loop(0, STEPS + 1, tick, 0)

    def result(half, c):
        target = out.at[pl.ds(half * W, W), pl.ds(c * C, C)]
        return pltpu.make_async_copy(XB.at[c] if half else RET.at[STEPS, c], target, osem.at[half, c])

    for c in range(2):
        result(1, c).start()
    for c in range(2):

        @pl.when(row > 0)
        def _():
            down(STEPS - 1, c).wait_recv()

        result(0, c).start()

    def finish_exchange(t, carry):
        for c in range(2):
            pl.when(row > 0)(lambda: up(t, c).wait_send())
            pl.when(row < ROWS - 1)(lambda: down(t, c).wait_send())
        return carry

    lax.fori_loop(0, STEPS, finish_exchange, 0)
    for half in range(2):
        for c in range(2):
            result(half, c).wait()


def local(vectors, reflectors):
    sem = pltpu.SemaphoreType.DMA
    anywhere = pl.BlockSpec(memory_space=pl.ANY)
    return pl.pallas_call(
        kernel,
        out_shape=jax.ShapeDtypeStruct(vectors.shape, F32),
        in_specs=[anywhere, anywhere],
        out_specs=anywhere,
        scratch_shapes=[
            pltpu.VMEM((UNITS, 2 * NX, NZ, 16, C), F32),
            pltpu.VMEM((UNITS, 2 * W, W), BF16),
            pltpu.VMEM((UNITS, 2 * W, W), BF16),
            pltpu.VMEM((UNITS, W, 2 * W), BF16),
            pltpu.VMEM((UNITS, W, 2 * W), BF16),
            pltpu.VMEM((STEPS + 1, 2, W, C), F32),
            pltpu.VMEM((STEPS + 1, 2, W, C), F32),
            pltpu.VMEM((STEPS, 2, W, C), F32),
            pltpu.VMEM((STEPS, 2, W, C), F32),
            pltpu.VMEM((2, W, C), F32),
            sem((6,)),
            sem((2, 2)),
            sem((3 * NZ,)),
            sem((3 * NZ,)),
            sem((UNITS, 13)),
            sem((UNITS, 13)),
            sem((STEPS, 2)),
            sem((STEPS, 2)),
            sem((STEPS, 2)),
            sem((STEPS, 2)),
        ],
        compiler_params=pltpu.CompilerParams(
            collective_id=0, has_side_effects=True, vmem_limit_bytes=56 * 2**20
        ),
    )(vectors, reflectors.reshape(UNITS, 16, W))


def solution(mesh):
    placed = (P("rows", "vecs"), P(None, "rows", "vecs", None))
    return jax.shard_map(
        local, mesh=mesh, in_specs=placed, out_specs=P("rows", "vecs"), check_vma=False
    )
```

```python
import jax
import jax.numpy as jnp
from jax import lax
from jax.experimental import pallas as pl
from jax.experimental.pallas import tpu as pltpu
from jax.sharding import PartitionSpec as P

F32, BF16 = jnp.float32, jnp.bfloat16
MESH = pl.DeviceIdType.MESH
STEPS, UNITS = 4, 8
W, C = 256, 128
NX, NZ = 4, 8
ROWS = 8


def split(value):
    high = value.astype(BF16)
    return high, (value - high.astype(F32)).astype(BF16)


def dot(a, b):
    return jnp.dot(a, b, preferred_element_type=F32)


def product(a, b):
    return dot(a[0], b[0]) + (dot(a[0], b[1]) + dot(a[1], b[0]))


def square(a, b):
    right = jnp.concatenate(
        [jnp.concatenate([b[0], b[1]], axis=1), jnp.concatenate([b[0], jnp.zeros_like(b[0])], axis=1)], axis=0
    )
    both = dot(jnp.concatenate([a[0], a[1]], axis=1), right)
    return both[:, :C] + both[:, C:]


NARROW = 32


def narrow_inverse(blocks):
    i = lax.broadcasted_iota(jnp.int32, (NARROW, C), 0)
    lane = lax.broadcasted_iota(jnp.int32, (NARROW, C), 1)
    j = lane % NARROW
    packs, accs = [], []
    for block in blocks:
        packed = block[:NARROW]
        for k in range(1, C // NARROW):
            packed = jnp.where(lane // NARROW == k, block[NARROW * k : NARROW * (k + 1)], packed)
        packs.append(jnp.where(i < j, packed, jnp.where(i == j, 0.5 * packed, 0.0)))
        accs.append(jnp.where(i == j, 1.0, 0.0))
    for k in range(NARROW - 1, -1, -1):
        live = 8 * (k // 8 + 1)
        for n in range(len(blocks)):
            column = jnp.take_along_axis(
                packs[n][:live], (lane - j + k)[:live], axis=1, mode="promise_in_bounds"
            )
            line = accs[n][k : k + 1] * (1.0 / column[k : k + 1])
            changed = jnp.where(i[:live] == k, line, accs[n][:live] - column * line)
            accs[n] = jnp.concatenate([changed, accs[n][live:]], axis=0) if live < NARROW else changed
    ri = lax.broadcasted_iota(jnp.int32, (C, C), 0)
    ci = lax.broadcasted_iota(jnp.int32, (C, C), 1)
    inside = ri // NARROW == ci // NARROW
    return [jnp.where(inside, jnp.concatenate([a] * (C // NARROW), axis=0), 0.0) for a in accs]


def widen(grams, inverses):
    ri = lax.broadcasted_iota(jnp.int32, (C, C), 0)
    ci = lax.broadcasted_iota(jnp.int32, (C, C), 1)
    above = ri // NARROW < ci // NARROW
    diagonals = [split(m) for m in inverses]
    nils = [split(square(d, split(jnp.where(above, g, 0.0)))) for d, g in zip(diagonals, grams)]
    twice = [split(square(n, n)) for n in nils]
    nears = [m - square(n, d) for m, n, d in zip(inverses, nils, diagonals)]
    return [p + square(q, split(p)) for p, q in zip(nears, twice)]


def kernel(
    vec, refl, out,
    G, VH, VL, ZH, ZL, RET, BEN, UPO, DNO, XB, SB,
    lsem, osem, fs, fr, gs, gr, us, ur, ds, dr,
):
    row = lax.axis_index("rows")
    v = lax.axis_index("vecs")
    x, z = v // NZ, lax.rem(v, NZ)

    def at_x(rel):
        return {"vecs": lax.rem(x + rel, NX) * NZ + z}

    turn = 1 - 2 * lax.rem(row, 2)

    def at_z(rel):
        return {"vecs": x * NZ + lax.rem(z + rel, NZ)}

    def local(i):
        if i < 2:
            return pltpu.make_async_copy(
                refl.at[:, :, pl.ds((1 - i) * C, C)], G.at[:, 2 * x + i, z], lsem.at[i]
            )
        half, c = (i - 2) // 2, (i - 2) % 2
        source = vec.at[pl.ds(half * W, W), pl.ds(c * C, C)]
        return pltpu.make_async_copy(source, XB.at[c] if half else RET.at[0, c], lsem.at[i])

    for i in range(6):
        local(i).start()

    barrier = pltpu.get_barrier_semaphore()
    for rel in (1, 2, 3):
        pl.semaphore_signal(barrier, inc=1, device_id=at_x(rel), device_id_type=MESH)
    for rel in range(1, NZ):
        pl.semaphore_signal(barrier, inc=1, device_id=at_z(rel), device_id_type=MESH)
    for rel in (1, ROWS - 1):
        beside = {"rows": lax.rem(row + rel, ROWS)}
        pl.semaphore_signal(barrier, inc=1, device_id=beside, device_id_type=MESH)
    for i in range(6):
        local(i).wait()
    pl.semaphore_wait(barrier, 12)

    def past_x(rel):
        return lax.rem(x + NX - rel, NX)

    def past_z(rel):
        return lax.rem(z + NZ - rel, NZ)

    def remote(slot, u, i, target):
        return pltpu.make_async_remote_copy(
            slot, slot, gs.at[u, i], gr.at[u, i], device_id=target, device_id_type=MESH
        )

    def xshard(u, rel, source):
        return remote(G.at[u, pl.ds(2 * source, 2), z], u, 6 + rel, at_x(rel))

    def zshard(u, rel, source):
        return remote(G.at[u, pl.ds(2 * x, 2), source], u, 5 + rel, at_z(rel))

    def xcolumn(u, i, side, rel, source):
        return remote(G.at[u, 2 * source + side], u, i, at_x(rel))

    def zrow(u, way, k, back):
        step = NZ + (turn if way == 0 else -turn)
        source = lax.rem(z + 5 * NZ - (step - NZ) * back, NZ)
        return remote(G.at[u, pl.ds(1, 7), source], u, k - 1 + 4 * way, at_z(step))

    HOPS = (4, 3)
    SIDES = tuple((side, rel) for rel in (1, 3, 2) for side in (1, 0))

    def unless_zero(side, source, run):
        if side == 1:
            run()
        else:
            pl.when(source != 0)(run)

    def by_row(u, k):
        if k == 0:
            for rel in (1, 3, 2):
                xshard(u, rel, past_x(rel)).wait_recv()
        for way in (0, 1):
            if 1 <= k <= HOPS[way]:
                zrow(u, way, k, k).wait_recv()
            if k < HOPS[way]:
                zrow(u, way, k + 1, k).start()

    def by_column(u, k):
        if k == 0:
            for rel in (1, 7, 2, 6, 3, 5, 4):
                zshard(u, rel, z).start()
        if k == 1:
            for rel in (1, 7, 2, 6, 3, 5, 4):
                zshard(u, rel, past_z(rel)).wait_recv()
            for i, (side, rel) in enumerate(SIDES):
                unless_zero(side, x, lambda: xcolumn(u, i, side, rel, x).start())
        if k == 2:
            for i, (side, rel) in enumerate(SIDES):
                unless_zero(side, past_x(rel), lambda: xcolumn(u, i, side, rel, past_x(rel)).wait_recv())

    def finish_by_row(u):
        for way in (0, 1):
            for k in range(1, HOPS[way] + 1):
                zrow(u, way, k, k - 1).wait_send()
        for rel in (1, 2, 3):
            xshard(u, rel, x).wait_send()

    def finish_by_column(u):
        for rel in range(1, NZ):
            zshard(u, rel, z).wait_send()
        for i, (side, rel) in enumerate(SIDES):
            unless_zero(side, x, lambda: xcolumn(u, i, side, rel, x).wait_send())

    ARRIVAL = (0, 1, 7, 2, 6, 3, 5, 4)

    def crossing(rel, along, source):
        i = 3 * along + rel - 1
        slot = G.at[0, pl.ds(2 * source, 2), past_z(along)]
        return pltpu.make_async_remote_copy(
            slot, slot, fs.at[i], fr.at[i], device_id=at_x(rel), device_id_type=MESH
        )

    for rel in (1, 3, 2):
        xshard(2, rel, x).start()
    by_column(0, 0)
    for rel in (1, 3, 2):
        crossing(rel, 0, x).start()
    by_row(2, 0)
    for along in ARRIVAL[1:]:
        zshard(0, along, past_z(along)).wait_recv()
        for rel in (1, 3, 2):
            crossing(rel, along, x).start()
    by_column(1, 0)
    for u in (4, 6):
        for rel in (1, 3, 2):
            xshard(u, rel, x).start()
    by_row(2, 1)
    by_column(3, 0)
    by_row(2, 2)
    for along in ARRIVAL:
        for rel in (1, 3, 2):
            crossing(rel, along, past_x(rel)).wait_recv()
    by_column(1, 1)

    def wave(s, events):
        for run, ahead, k in events:
            taken = (s + ahead < UNITS) & (s > 0) if (ahead, k) in ((2, 3),) else s + ahead < UNITS
            pl.when(taken)(lambda: run(s + ahead, k))

    AFTER_EVEN = ((by_row, 2, 3), (by_row, 4, 1), (by_column, 3, 1), (by_column, 5, 0), (by_column, 1, 2))
    AFTER_ODD = ((by_row, 3, 2), (by_row, 5, 0), (by_row, 1, 4))

    def prepare(u):
        left = jnp.concatenate([G[u, 2 * i + 1].reshape(C, C) for i in range(NX)], axis=0)
        right = jnp.concatenate(
            [jnp.zeros((C, C), F32)] + [G[u, 2 * i].reshape(C, C) for i in range(1, NX)], axis=0
        )
        vh, vl = split(jnp.concatenate([left, right], axis=1))
        th, tl = vh.T, vl.T
        VH[u], VL[u] = vh, vl
        upper = product((th[:C], tl[:C]), (vh, vl))
        both = dot(th[C:, C:], jnp.concatenate([vh[C:, C:], vl[C:, C:]], axis=1))
        lower = both[:, :C] + (both[:, C:] + dot(tl[C:, C:], vh[C:, C:]))
        grams = [upper[:, :C], lower]
        inverses = widen(grams, narrow_inverse(grams))
        (ah, al), (ch, cl) = split(inverses[0]), split(inverses[1])
        corner = square((ah, al), split(square(split(upper[:, C:]), (ch, cl))))
        bh, bl = split(-corner)
        wide = (jnp.concatenate([ah, bh], axis=1), jnp.concatenate([al, bl], axis=1))
        ZH[u, :C], ZL[u, :C] = split(product(wide, (th, tl)))
        ZH[u, C:], ZL[u, C:] = split(
            dot(jnp.concatenate([ch, cl], axis=1), jnp.concatenate([th[C:], th[C:]], axis=0)) + dot(ch, tl[C:])
        )

    def up(t, c):
        return pltpu.make_async_remote_copy(
            UPO.at[t, c], BEN.at[t, c], us.at[t, c], ur.at[t, c],
            device_id={"rows": lax.rem(row + ROWS - 1, ROWS)}, device_id_type=MESH,
        )

    def down(t, c):
        return pltpu.make_async_remote_copy(
            DNO.at[t, c], RET.at[t + 1, c], ds.at[t, c], dr.at[t, c],
            device_id={"rows": lax.rem(row + 1, ROWS)}, device_id_type=MESH,
        )

    def part(u, start, rows):
        high, low = split(rows)
        wide = dot(ZH[u, :, start : start + W], jnp.concatenate([high, low], axis=1))
        return wide[:, :C] + (wide[:, C:] + dot(ZL[u, :, start : start + W], high))

    def change(u, start, solved):
        wide = dot(VH[u, start : start + W], jnp.concatenate(solved, axis=1))
        return wide[:, :C] + (wide[:, C:] + dot(VL[u, start : start + W], solved[0]))

    def even(t):
        u = 2 * t
        for c in range(2):
            SB[c] = part(u, W, XB[c])

        for c in range(2):

            @pl.when((row > 0) & (t > 0))
            def _():
                down(t - 1, c).wait_recv()

            top, bottom = RET[t, c], XB[c]
            solved = split(SB[c] + part(u, 0, top))
            top = top - change(u, 0, solved)

            @pl.when(row > 0)
            def _():
                UPO[t, c] = top
                up(t, c).start()

            @pl.when(row == 0)
            def _():
                RET[t + 1, c] = top

            XB[c] = bottom - change(u, W, solved)

    def odd(t):
        u = 2 * t + 1
        for c in range(2):
            SB[c] = part(u, 0, XB[c])

        for c in range(2):

            @pl.when(row < ROWS - 1)
            def _():
                up(t, c).wait_recv()

            top, bottom = XB[c], BEN[t, c]
            solved = split(SB[c] + part(u, W, bottom))
            bottom = bottom - change(u, W, solved)

            @pl.when(row < ROWS - 1)
            def _():
                DNO[t, c] = bottom
                down(t, c).start()

            @pl.when(row == ROWS - 1)
            def _():
                BEN[t + 1, c] = bottom

            XB[c] = top - change(u, 0, solved)

    @pl.when(row == ROWS - 1)
    def _():
        BEN[0] = jnp.zeros((2, W, C), F32)

    def finish_first():
        for along in range(NZ):
            if along:
                zshard(0, along, z).wait_send()
            for rel in (1, 2, 3):
                crossing(rel, along, x).wait_send()

    def finish_gather(t, carry):
        pl.when(t == 0)(finish_first)
        pl.when(t != 0)(lambda: finish_by_row(2 * t))
        finish_by_column(2 * t + 1)
        return carry

    def tick(t, carry):
        pl.when(t > 0)(lambda: even(t - 1))

        @pl.when(t > 0)
        def _():
            wave(2 * t - 2, AFTER_EVEN)
            prepare(2 * t - 1)

        @pl.when(t == STEPS)
        def _():
            lax.fori_loop(0, STEPS, finish_gather, 0)

        pl.when(t > 0)(lambda: odd(t - 1))

        @pl.when(t < STEPS)
        def _():
            pl.when(t > 0)(lambda: wave(2 * t - 1, AFTER_ODD))
            prepare(2 * t)

        @pl.when(t == 0)
        def _():
            by_row(2, 3)
            by_row(4, 0)

        return carry

    lax.fori_loop(0, STEPS + 1, tick, 0)

    def result(half, c):
        target = out.at[pl.ds(half * W, W), pl.ds(c * C, C)]
        return pltpu.make_async_copy(XB.at[c] if half else RET.at[STEPS, c], target, osem.at[half, c])

    for c in range(2):
        result(1, c).start()
    for c in range(2):

        @pl.when(row > 0)
        def _():
            down(STEPS - 1, c).wait_recv()

        result(0, c).start()

    def finish_exchange(t, carry):
        for c in range(2):
            pl.when(row > 0)(lambda: up(t, c).wait_send())
            pl.when(row < ROWS - 1)(lambda: down(t, c).wait_send())
        return carry

    lax.fori_loop(0, STEPS, finish_exchange, 0)
    for half in range(2):
        for c in range(2):
            result(half, c).wait()


def local(vectors, reflectors):
    sem = pltpu.SemaphoreType.DMA
    anywhere = pl.BlockSpec(memory_space=pl.ANY)
    return pl.pallas_call(
        kernel,
        out_shape=jax.ShapeDtypeStruct(vectors.shape, F32),
        in_specs=[anywhere, anywhere],
        out_specs=anywhere,
        scratch_shapes=[
            pltpu.VMEM((UNITS, 2 * NX, NZ, 16, C), F32),
            pltpu.VMEM((UNITS, 2 * W, W), BF16),
            pltpu.VMEM((UNITS, 2 * W, W), BF16),
            pltpu.VMEM((UNITS, W, 2 * W), BF16),
            pltpu.VMEM((UNITS, W, 2 * W), BF16),
            pltpu.VMEM((STEPS + 1, 2, W, C), F32),
            pltpu.VMEM((STEPS + 1, 2, W, C), F32),
            pltpu.VMEM((STEPS, 2, W, C), F32),
            pltpu.VMEM((STEPS, 2, W, C), F32),
            pltpu.VMEM((2, W, C), F32),
            pltpu.VMEM((2, W, C), F32),
            sem((6,)),
            sem((2, 2)),
            sem((3 * NZ,)),
            sem((3 * NZ,)),
            sem((UNITS, 13)),
            sem((UNITS, 13)),
            sem((STEPS, 2)),
            sem((STEPS, 2)),
            sem((STEPS, 2)),
            sem((STEPS, 2)),
        ],
        compiler_params=pltpu.CompilerParams(
            collective_id=0, has_side_effects=True, vmem_limit_bytes=56 * 2**20
        ),
    )(vectors, reflectors.reshape(UNITS, 16, W))


def solution(mesh):
    placed = (P("rows", "vecs"), P(None, "rows", "vecs", None))
    return jax.shard_map(
        local, mesh=mesh, in_specs=placed, out_specs=P("rows", "vecs"), check_vma=False
    )
```

```python
import jax
import jax.numpy as jnp
from jax import lax
from jax.experimental import pallas as pl
from jax.experimental.pallas import tpu as pltpu
from jax.sharding import PartitionSpec as P

F32, BF16 = jnp.float32, jnp.bfloat16
MESH = pl.DeviceIdType.MESH
STEPS, UNITS = 4, 8
W, C = 256, 128
NX, NZ = 4, 8
ROWS = 8


def split(value):
    high = value.astype(BF16)
    return high, (value - high.astype(F32)).astype(BF16)


def dot(a, b):
    return jnp.dot(a, b, preferred_element_type=F32)


def product(a, b):
    return dot(a[0], b[0]) + (dot(a[0], b[1]) + dot(a[1], b[0]))


def square(a, b):
    right = jnp.concatenate(
        [jnp.concatenate([b[0], b[1]], axis=1), jnp.concatenate([b[0], jnp.zeros_like(b[0])], axis=1)], axis=0
    )
    both = dot(jnp.concatenate([a[0], a[1]], axis=1), right)
    return both[:, :C] + both[:, C:]


NARROW = 32


def narrow_inverse(blocks):
    i = lax.broadcasted_iota(jnp.int32, (NARROW, C), 0)
    lane = lax.broadcasted_iota(jnp.int32, (NARROW, C), 1)
    j = lane % NARROW
    packs, accs = [], []
    for block in blocks:
        packed = block[:NARROW]
        for k in range(1, C // NARROW):
            packed = jnp.where(lane // NARROW == k, block[NARROW * k : NARROW * (k + 1)], packed)
        packs.append(jnp.where(i < j, packed, jnp.where(i == j, 0.5 * packed, 0.0)))
        accs.append(jnp.where(i == j, 1.0, 0.0))
    for k in range(NARROW - 1, -1, -1):
        live = 8 * (k // 8 + 1)
        for n in range(len(blocks)):
            column = jnp.take_along_axis(
                packs[n][:live], (lane - j + k)[:live], axis=1, mode="promise_in_bounds"
            )
            line = accs[n][k : k + 1] * (1.0 / column[k : k + 1])
            changed = jnp.where(i[:live] == k, line, accs[n][:live] - column * line)
            accs[n] = jnp.concatenate([changed, accs[n][live:]], axis=0) if live < NARROW else changed
    ri = lax.broadcasted_iota(jnp.int32, (C, C), 0)
    ci = lax.broadcasted_iota(jnp.int32, (C, C), 1)
    inside = ri // NARROW == ci // NARROW
    return [jnp.where(inside, jnp.concatenate([a] * (C // NARROW), axis=0), 0.0) for a in accs]


def widen(grams, inverses):
    ri = lax.broadcasted_iota(jnp.int32, (C, C), 0)
    ci = lax.broadcasted_iota(jnp.int32, (C, C), 1)
    above = ri // NARROW < ci // NARROW
    diagonals = [split(m) for m in inverses]
    nils = [split(square(d, split(jnp.where(above, g, 0.0)))) for d, g in zip(diagonals, grams)]
    twice = [split(square(n, n)) for n in nils]
    nears = [m - square(n, d) for m, n, d in zip(inverses, nils, diagonals)]
    return [p + square(q, split(p)) for p, q in zip(nears, twice)]


def kernel(
    vec, refl, out,
    G, VH, VL, ZH, ZL, RET, BEN, UPO, DNO, XB,
    lsem, osem, fs, fr, gs, gr, us, ur, ds, dr,
):
    row = lax.axis_index("rows")
    v = lax.axis_index("vecs")
    x, z = v // NZ, lax.rem(v, NZ)

    def at_x(rel):
        return {"vecs": lax.rem(x + rel, NX) * NZ + z}

    turn = 1 - 2 * lax.rem(row, 2)

    def at_z(rel):
        return {"vecs": x * NZ + lax.rem(z + rel, NZ)}

    def local(i):
        if i < 2:
            return pltpu.make_async_copy(
                refl.at[:, :, pl.ds((1 - i) * C, C)], G.at[:, 2 * x + i, z], lsem.at[i]
            )
        half, c = (i - 2) // 2, (i - 2) % 2
        source = vec.at[pl.ds(half * W, W), pl.ds(c * C, C)]
        return pltpu.make_async_copy(source, XB.at[c] if half else RET.at[0, c], lsem.at[i])

    for i in range(6):
        local(i).start()

    barrier = pltpu.get_barrier_semaphore()
    for rel in (1, 2, 3):
        pl.semaphore_signal(barrier, inc=1, device_id=at_x(rel), device_id_type=MESH)
    for rel in range(1, NZ):
        pl.semaphore_signal(barrier, inc=1, device_id=at_z(rel), device_id_type=MESH)
    for rel in (1, ROWS - 1):
        beside = {"rows": lax.rem(row + rel, ROWS)}
        pl.semaphore_signal(barrier, inc=1, device_id=beside, device_id_type=MESH)
    for i in range(6):
        local(i).wait()
    pl.semaphore_wait(barrier, 12)

    def past_x(rel):
        return lax.rem(x + NX - rel, NX)

    def past_z(rel):
        return lax.rem(z + NZ - rel, NZ)

    def remote(slot, u, i, target):
        return pltpu.make_async_remote_copy(
            slot, slot, gs.at[u, i], gr.at[u, i], device_id=target, device_id_type=MESH
        )

    def xshard(u, rel, source):
        return remote(G.at[u, pl.ds(2 * source, 2), z], u, 6 + rel, at_x(rel))

    def zshard(u, rel, source):
        return remote(G.at[u, pl.ds(2 * x, 2), source], u, 5 + rel, at_z(rel))

    def xcolumn(u, i, side, rel, source):
        return remote(G.at[u, 2 * source + side], u, i, at_x(rel))

    def zrow(u, way, k, back):
        step = NZ + (turn if way == 0 else -turn)
        source = lax.rem(z + 5 * NZ - (step - NZ) * back, NZ)
        return remote(G.at[u, pl.ds(1, 7), source], u, k - 1 + 4 * way, at_z(step))

    HOPS = (4, 3)
    SIDES = tuple((side, rel) for rel in (1, 3, 2) for side in (1, 0))

    def unless_zero(side, source, run):
        if side == 1:
            run()
        else:
            pl.when(source != 0)(run)

    def by_row(u, k):
        if k == 0:
            for rel in (1, 3, 2):
                xshard(u, rel, past_x(rel)).wait_recv()
        for way in (0, 1):
            if 1 <= k <= HOPS[way]:
                zrow(u, way, k, k).wait_recv()
            if k < HOPS[way]:
                zrow(u, way, k + 1, k).start()

    def by_column(u, k):
        if k == 0:
            for rel in (1, 7, 2, 6, 3, 5, 4):
                zshard(u, rel, z).start()
        if k == 1:
            for rel in (1, 7, 2, 6, 3, 5, 4):
                zshard(u, rel, past_z(rel)).wait_recv()
            for i, (side, rel) in enumerate(SIDES):
                unless_zero(side, x, lambda: xcolumn(u, i, side, rel, x).start())
        if k == 2:
            for i, (side, rel) in enumerate(SIDES):
                unless_zero(side, past_x(rel), lambda: xcolumn(u, i, side, rel, past_x(rel)).wait_recv())

    def finish_by_row(u):
        for way in (0, 1):
            for k in range(1, HOPS[way] + 1):
                zrow(u, way, k, k - 1).wait_send()
        for rel in (1, 2, 3):
            xshard(u, rel, x).wait_send()

    def finish_by_column(u):
        for rel in range(1, NZ):
            zshard(u, rel, z).wait_send()
        for i, (side, rel) in enumerate(SIDES):
            unless_zero(side, x, lambda: xcolumn(u, i, side, rel, x).wait_send())

    ARRIVAL = (0, 1, 7, 2, 6, 3, 5, 4)

    def crossing(rel, along, source):
        i = 3 * along + rel - 1
        slot = G.at[0, pl.ds(2 * source, 2), past_z(along)]
        return pltpu.make_async_remote_copy(
            slot, slot, fs.at[i], fr.at[i], device_id=at_x(rel), device_id_type=MESH
        )

    for rel in (1, 3, 2):
        xshard(2, rel, x).start()
    by_column(0, 0)
    for rel in (1, 3, 2):
        crossing(rel, 0, x).start()
    by_row(2, 0)
    for along in ARRIVAL[1:]:
        zshard(0, along, past_z(along)).wait_recv()
        for rel in (1, 3, 2):
            crossing(rel, along, x).start()
    by_column(1, 0)
    for u in (4, 6):
        for rel in (1, 3, 2):
            xshard(u, rel, x).start()
    by_row(2, 1)
    by_column(3, 0)
    by_row(2, 2)
    for along in ARRIVAL:
        for rel in (1, 3, 2):
            crossing(rel, along, past_x(rel)).wait_recv()
    by_column(1, 1)

    def wave(s, events):
        for run, ahead, k in events:
            taken = (s + ahead < UNITS) & (s > 0) if (ahead, k) in ((2, 3),) else s + ahead < UNITS
            pl.when(taken)(lambda: run(s + ahead, k))

    AFTER_EVEN = ((by_row, 2, 3), (by_row, 4, 1), (by_column, 3, 1), (by_column, 5, 0), (by_column, 1, 2))
    AFTER_ODD = ((by_row, 3, 2), (by_row, 5, 0), (by_row, 1, 4))

    def prepare(u):
        left = jnp.concatenate([G[u, 2 * i + 1].reshape(C, C) for i in range(NX)], axis=0)
        right = jnp.concatenate(
            [jnp.zeros((C, C), F32)] + [G[u, 2 * i].reshape(C, C) for i in range(1, NX)], axis=0
        )
        vh, vl = split(jnp.concatenate([left, right], axis=1))
        th, tl = vh.T, vl.T
        VH[u], VL[u] = vh, vl
        upper = product((th[:C], tl[:C]), (vh, vl))
        both = dot(th[C:, C:], jnp.concatenate([vh[C:, C:], vl[C:, C:]], axis=1))
        lower = both[:, :C] + (both[:, C:] + dot(tl[C:, C:], vh[C:, C:]))
        grams = [upper[:, :C], lower]
        inverses = widen(grams, narrow_inverse(grams))
        (ah, al), (ch, cl) = split(inverses[0]), split(inverses[1])
        middle = split(square((ah, al), split(upper[:, C:])))
        zh, zl = split(
            dot(jnp.concatenate([ch, cl], axis=1), jnp.concatenate([th[C:], th[C:]], axis=0)) + dot(ch, tl[C:])
        )
        ZH[u, C:], ZL[u, C:] = zh, zl
        head = product((ah, al), (th[:C], tl[:C]))
        ZH[u, :C], ZL[u, :C] = split(head - product(middle, (zh, zl)))

    def up(t, c):
        return pltpu.make_async_remote_copy(
            UPO.at[t, c], BEN.at[t, c], us.at[t, c], ur.at[t, c],
            device_id={"rows": lax.rem(row + ROWS - 1, ROWS)}, device_id_type=MESH,
        )

    def down(t, c):
        return pltpu.make_async_remote_copy(
            DNO.at[t, c], RET.at[t + 1, c], ds.at[t, c], dr.at[t, c],
            device_id={"rows": lax.rem(row + 1, ROWS)}, device_id_type=MESH,
        )

    def solved_of(u, top, bottom):
        (th, tl), (bh, bl) = split(top), split(bottom)
        rh = jnp.concatenate([th, bh], axis=0)
        rl = jnp.concatenate([tl, bl], axis=0)
        wide = dot(ZH[u], jnp.concatenate([rh, rl], axis=1))
        return split(wide[:, :C] + (wide[:, C:] + dot(ZL[u], rh)))

    def change(u, start, solved):
        wide = dot(VH[u, start : start + W], jnp.concatenate(solved, axis=1))
        return wide[:, :C] + (wide[:, C:] + dot(VL[u, start : start + W], solved[0]))

    def even(t):
        u = 2 * t
        for c in range(2):

            @pl.when((row > 0) & (t > 0))
            def _():
                down(t - 1, c).wait_recv()

            top, bottom = RET[t, c], XB[c]
            solved = solved_of(u, top, bottom)
            top = top - change(u, 0, solved)

            @pl.when(row > 0)
            def _():
                UPO[t, c] = top
                up(t, c).start()

            @pl.when(row == 0)
            def _():
                RET[t + 1, c] = top

            XB[c] = bottom - change(u, W, solved)

    def odd(t):
        u = 2 * t + 1
        for c in range(2):

            @pl.when(row < ROWS - 1)
            def _():
                up(t, c).wait_recv()

            top, bottom = XB[c], BEN[t, c]
            solved = solved_of(u, top, bottom)
            bottom = bottom - change(u, W, solved)

            @pl.when(row < ROWS - 1)
            def _():
                DNO[t, c] = bottom
                down(t, c).start()

            @pl.when(row == ROWS - 1)
            def _():
                BEN[t + 1, c] = bottom

            XB[c] = top - change(u, 0, solved)

    @pl.when(row == ROWS - 1)
    def _():
        BEN[0] = jnp.zeros((2, W, C), F32)

    def finish_first():
        for along in range(NZ):
            if along:
                zshard(0, along, z).wait_send()
            for rel in (1, 2, 3):
                crossing(rel, along, x).wait_send()

    def finish_gather(t, carry):
        pl.when(t == 0)(finish_first)
        pl.when(t != 0)(lambda: finish_by_row(2 * t))
        finish_by_column(2 * t + 1)
        return carry

    def tick(t, carry):
        pl.when(t > 0)(lambda: even(t - 1))

        @pl.when(t > 0)
        def _():
            wave(2 * t - 2, AFTER_EVEN)
            prepare(2 * t - 1)

        @pl.when(t == STEPS)
        def _():
            lax.fori_loop(0, STEPS, finish_gather, 0)

        pl.when(t > 0)(lambda: odd(t - 1))

        @pl.when(t < STEPS)
        def _():
            pl.when(t > 0)(lambda: wave(2 * t - 1, AFTER_ODD))
            prepare(2 * t)

        @pl.when(t == 0)
        def _():
            by_row(2, 3)
            by_row(4, 0)

        return carry

    lax.fori_loop(0, STEPS + 1, tick, 0)

    def result(half, c):
        target = out.at[pl.ds(half * W, W), pl.ds(c * C, C)]
        return pltpu.make_async_copy(XB.at[c] if half else RET.at[STEPS, c], target, osem.at[half, c])

    for c in range(2):
        result(1, c).start()
    for c in range(2):

        @pl.when(row > 0)
        def _():
            down(STEPS - 1, c).wait_recv()

        result(0, c).start()

    def finish_exchange(t, carry):
        for c in range(2):
            pl.when(row > 0)(lambda: up(t, c).wait_send())
            pl.when(row < ROWS - 1)(lambda: down(t, c).wait_send())
        return carry

    lax.fori_loop(0, STEPS, finish_exchange, 0)
    for half in range(2):
        for c in range(2):
            result(half, c).wait()


def local(vectors, reflectors):
    sem = pltpu.SemaphoreType.DMA
    anywhere = pl.BlockSpec(memory_space=pl.ANY)
    return pl.pallas_call(
        kernel,
        out_shape=jax.ShapeDtypeStruct(vectors.shape, F32),
        in_specs=[anywhere, anywhere],
        out_specs=anywhere,
        scratch_shapes=[
            pltpu.VMEM((UNITS, 2 * NX, NZ, 16, C), F32),
            pltpu.VMEM((UNITS, 2 * W, W), BF16),
            pltpu.VMEM((UNITS, 2 * W, W), BF16),
            pltpu.VMEM((UNITS, W, 2 * W), BF16),
            pltpu.VMEM((UNITS, W, 2 * W), BF16),
            pltpu.VMEM((STEPS + 1, 2, W, C), F32),
            pltpu.VMEM((STEPS + 1, 2, W, C), F32),
            pltpu.VMEM((STEPS, 2, W, C), F32),
            pltpu.VMEM((STEPS, 2, W, C), F32),
            pltpu.VMEM((2, W, C), F32),
            sem((6,)),
            sem((2, 2)),
            sem((3 * NZ,)),
            sem((3 * NZ,)),
            sem((UNITS, 13)),
            sem((UNITS, 13)),
            sem((STEPS, 2)),
            sem((STEPS, 2)),
            sem((STEPS, 2)),
            sem((STEPS, 2)),
        ],
        compiler_params=pltpu.CompilerParams(
            collective_id=0, has_side_effects=True, vmem_limit_bytes=56 * 2**20
        ),
    )(vectors, reflectors.reshape(UNITS, 16, W))


def solution(mesh):
    placed = (P("rows", "vecs"), P(None, "rows", "vecs", None))
    return jax.shard_map(
        local, mesh=mesh, in_specs=placed, out_specs=P("rows", "vecs"), check_vma=False
    )
```
